512 devices in a mesh: row: 16 (over y_lo, x, core), col: 32 (over z, y_hi).
Axes of the slice: x: 4, y: 4 (y_hi: 2, y_lo: 2; y = y_hi * 2 + y_lo), z: 16, core: 2. Of those that a mesh axis runs over, the one named last changes fastest.
Arguments:
- activations: bfloat16 [512, 28672], P('row', 'col'), may hold values from -160 to 160
- down_weight: bfloat16 [28672, 256], P(('row', 'col')), may hold values from -6 to 6
- keep_mask: int32 [28672, 256], P(('row', 'col')), may hold values 0 or 1
Outputs:
- gram_damped: bfloat16 [28672, 28672], P('row', 'col')
- updated: bfloat16 [28672, 256], P(('row', 'col'))
The draws below stay inside these ranges and needn't reach their ends.
All inputs are finite; a program needn't handle non-finite values. No bound on the sum of `keep_mask` on one device may be relied on, other than what follows from the above.
Results may differ from the reference program's by a relative error of at most 0.017.
Values may be sent and summed in bfloat16 or wider, within the bound.
A program may use at most 64 MiB of HBM per device.

```python
import jax
import jax.numpy as jnp
from jax import lax

FF = 28672
ROWS = 512
OUT = 256
N_ROW = 16


def draw_activations(key, part):
    keys = jax.random.split(jax.random.fold_in(key, 17), 3)
    col_scale = jnp.exp(jax.random.uniform(keys[0], (FF,), jnp.float32, -1.15, 1.15) + 0.55 * jnp.linspace(-1.0, 1.0, FF))
    row_scale = jnp.exp(jax.random.uniform(keys[1], (ROWS,), jnp.float32, -0.35, 0.35) + 0.275 * jnp.linspace(-1.0, 1.0, ROWS))
    values = jnp.clip(jax.random.normal(keys[2], (ROWS, FF), jnp.float32), -4.0, 4.0)
    return (row_scale[:, None] * col_scale[None, :] * values).astype(jnp.bfloat16)


def set_ends(values, rng, low, top_value):
    longest = values.shape.index(max(values.shape))
    spots = []
    for shift in (0, 1):
        where = [jax.random.randint(jax.random.fold_in(rng, axis), (), 0, length) for axis, length in enumerate(values.shape)]
        where[longest] = (where[longest] + shift) % values.shape[longest]
        spots.append(tuple(where))
    return values.at[spots[0]].set(low).at[spots[1]].set(top_value)


def level_of(stream_key, dims, cuts, smallest, largest):
    gain, own = 1.0, jax.random.fold_in(stream_key, 6)
    for position, parts in cuts:
        heights = jnp.exp(jax.random.uniform(jax.random.fold_in(own, position), (parts,), jnp.float32, smallest / len(cuts), largest / len(cuts)))
        gain = gain * jnp.repeat(heights, dims[position] // parts).reshape([-1 if axis == position else 1 for axis in range(len(dims))])
    return gain


def bell_draw(own_key, shape, deviation, limit, pieces=(), held_as=jnp.bfloat16):
    drawn = jax.random.normal(own_key, shape, jnp.float32) * deviation
    if len(pieces) > 0:
        drawn = level_of(own_key, shape, pieces, -0.22, 0.18) * drawn
    return jnp.clip(drawn, min=-limit, max=limit).astype(held_as)


def setup_inputs(seed: int = 0) -> dict:
    key_list = jax.random.split(jax.random.key(seed), 4)
    activations = draw_activations(jax.random.fold_in(key_list[3], 71), 0)
    down_weight = bell_draw(key_list[1], (FF, OUT), 1.0, 6.0, ((0, 512),))
    keep_mask = set_ends((jax.random.randint(key_list[2], (FF, OUT), 0, 2) < 1).astype(jnp.int32), jax.random.fold_in(key_list[2], 1), 0, 1)
    return dict(activations=activations, down_weight=down_weight, keep_mask=keep_mask)


damp_ratio = 0.1
step_ratio = 0.25


def reference(activations, down_weight, keep_mask):
    act_float = activations.astype(jnp.float32)
    mean_square = jnp.sum(act_float * act_float) / (ROWS * FF) + 1e-6
    damping = damp_ratio * mean_square
    pruned = down_weight * (1 - keep_mask).astype(jnp.bfloat16)
    pruned_float = pruned.astype(jnp.float32)
    block_rows = FF // N_ROW

    def one_block(block_index):
        start = (block_index * block_rows).astype(jnp.int32)
        slab = lax.dynamic_slice_in_dim(activations, start, block_rows, 1)
        gram_rows = lax.dot_general(slab, activations, (((0,), (0,)), ((), ())), preferred_element_type=jnp.float32) / ROWS
        global_rows = start + lax.iota(jnp.int32, block_rows)
        global_cols = lax.iota(jnp.int32, FF)
        damped = gram_rows + jnp.where(global_rows[:, None] == global_cols[None, :], damping, jnp.float32(0.0))
        descent = jnp.dot(gram_rows, pruned_float, precision=lax.Precision.HIGHEST)
        return damped.astype(jnp.bfloat16), descent

    gram_blocks, descents = lax.map(one_block, jnp.arange(N_ROW, dtype=jnp.int32))
    gram_damped = gram_blocks.reshape(FF, FF)
    descent = descents.reshape(FF, OUT)
    keep_float = keep_mask.astype(jnp.float32)
    updated = keep_float * (down_weight.astype(jnp.float32) + step_ratio * descent / ((1.0 + damp_ratio) * mean_square))
    return gram_damped, updated.astype(jnp.bfloat16)
```

```python
import functools

import jax
import jax.numpy as jnp
from jax import lax
from jax.experimental import pallas as pl
from jax.experimental.pallas import tpu as pltpu
from jax.sharding import Mesh
from jax.sharding import PartitionSpec as P

MESH = pl.DeviceIdType.MESH
AXES = ("row_0", "row_1", "row_2", "col_0", "col_1")
ROW = AXES[:3]
COL = AXES[3:]
F32 = jnp.float32
BF16 = jnp.bfloat16
SUB = 2

damp_ratio = 0.1
step_ratio = 0.25


def exchange_kernel(
    nx,
    nz,
    a_ref,
    dw_ref,
    mask_ref,
    rowp_ref,
    colp_ref,
    s_ref,
    q_ref,
    zbuf,
    pown,
    pbuf,
    pfull,
    spart,
    yx_send,
    yx_recv,
    yq_send,
    yq_recv,
    zs_buf,
    zq_buf,
    ring_send,
    ring_recv,
    row_send,
    row_recv,
    col_send,
    col_recv,
    perm_sem,
    pag_send,
    pag_recv,
    yx_sem,
    zs_send,
    zs_recv,
    zq_send,
    zq_recv,
    pln_send,
    pln_recv,
):
    nr = 4 * nx
    own = dw_ref.shape[0]
    rows, width = a_ref.shape
    half = rows // 2
    sub_rows = rows // SUB
    yl, x, k, z, yh = (lax.axis_index(name) for name in AXES)
    r = (yl * nx + x) * 2 + k
    chip = yl * nx + x
    plane = 2 * r + yh

    def dev(r_, z_, yh_):
        return dict(
            row_0=lax.div(r_, 2 * nx),
            row_1=lax.rem(lax.div(r_, 2), nx),
            row_2=lax.rem(r_, 2),
            col_0=z_,
            col_1=yh_,
        )

    def remote(src, dst, send, recv, to):
        return pltpu.make_async_remote_copy(
            src_ref=src, dst_ref=dst, send_sem=send, recv_sem=recv, device_id=to, device_id_type=MESH
        )

    t_r, t_z, t_yh = 2 * lax.rem(z, nz // 2) + yh, r, lax.div(z, nz // 2)
    s_r, s_z, s_yh = z, yh * (nz // 2) + lax.div(r, 2), lax.rem(r, 2)
    fixed = (t_r == r) & (t_z == z) & (t_yh == yh)

    barrier = pltpu.get_barrier_semaphore()

    def greet(to):
        pl.semaphore_signal(barrier, inc=1, device_id=to, device_id_type=MESH)

    greet(dev(t_r, t_z, t_yh))
    greet(dev(s_r, s_z, s_yh))
    for off in range(1, nz):
        greet(dev(r, lax.rem(z + off, nz), yh))
    for off in range(1, 2 * nr):
        other = lax.rem(plane + off, 2 * nr)
        greet(dev(lax.div(other, 2), z, lax.rem(other, 2)))

    pown[0:own, :] = dw_ref[...] * (1 - mask_ref[...]).astype(BF16)
    act = a_ref[...].astype(F32)
    square = jnp.sum(jnp.sum(act * act, axis=0, keepdims=True), axis=1, keepdims=True)
    square = jnp.broadcast_to(square, (8, 256))
    high = square.astype(BF16).astype(F32)
    middle = (square - high).astype(BF16).astype(F32)
    low = (square - high - middle).astype(BF16).astype(F32)
    line = lax.broadcasted_iota(jnp.int32, (8, 256), 0)
    zero = jnp.zeros((8, 256), F32)
    coded = jnp.where(line == 0, high, jnp.where(line == 1, middle, jnp.where(line == 2, low, zero)))
    pown[own : own + 8, :] = coded.astype(BF16)

    pl.semaphore_wait(barrier, 2 + (nz - 1) + (2 * nr - 1))

    perm = remote(pown, pbuf.at[r], perm_sem.at[0], perm_sem.at[1], dev(t_r, t_z, t_yh))
    perm_out = remote(pown, pbuf.at[t_r], perm_sem.at[0], perm_sem.at[1], dev(t_r, t_z, t_yh))
    perm_here = pltpu.make_async_copy(pown, pbuf.at[r], perm_sem.at[1])

    @pl.when(jnp.logical_not(fixed))
    def _():
        perm_out.start()

    @pl.when(fixed)
    def _():
        perm_here.start()

    plus, minus = lax.rem(z + 1, nz), lax.rem(z + nz - 1, nz)
    hops = (nz // 2, nz - 1 - nz // 2)

    def ring_block(way, step):
        return lax.rem(z - step + nz, nz) if way == 0 else lax.rem(z + step, nz)

    def piece(block, step, sub):
        if step == 0:
            return a_ref.at[pl.ds(sub * sub_rows, sub_rows)]
        return zbuf.at[block, sub]

    def ring_copy(way, step, sub):
        block = ring_block(way, step)
        to = plus if way == 0 else minus
        return remote(
            piece(block, step, sub),
            zbuf.at[block, sub],
            ring_send.at[way, step, sub],
            ring_recv.at[way, step, sub],
            dev(r, to, yh),
        )

    def row_copy(block, step, to_yh, sub):
        return remote(
            piece(block, step, sub),
            rowp_ref.at[yh, r, sub],
            row_send.at[block, to_yh, sub],
            row_recv.at[yh, r, sub],
            dev(block, z, to_yh),
        )

    def row_local(block, step, sub):
        return pltpu.make_async_copy(piece(block, step, sub), rowp_ref.at[yh, r, sub], row_recv.at[yh, r, sub])

    def row_start(block, step, sub):
        for to_yh in range(2):
            here = (block == r) & (yh == to_yh)

            @pl.when(jnp.logical_not(here))
            def _():
                row_copy(block, step, to_yh, sub).start()

            @pl.when(here)
            def _():
                row_local(block, step, sub).start()

    def col_copy(off):
        other = lax.rem(chip + off, 2 * nx)
        return remote(a_ref, colp_ref.at[r], col_send.at[off], col_recv.at[r], dev(2 * other + k, z, yh))

    def col_from(off):
        return 2 * lax.rem(chip - off + 2 * nx, 2 * nx) + k

    def col_wait(source):
        remote(a_ref, colp_ref.at[source], col_send.at[0], col_recv.at[source], dev(r, z, yh)).wait_recv()

    def col_pass(off):
        source = col_from(off)
        src = a_ref if off == 0 else colp_ref.at[source]
        return remote(src, colp_ref.at[source], col_send.at[2 * nx + off], col_recv.at[source], dev(2 * chip + 1 - k, z, yh))

    col_own = pltpu.make_async_copy(a_ref, colp_ref.at[r], col_recv.at[r])

    for sub in range(SUB):
        for way in range(2):
            ring_copy(way, 0, sub).start()
    for sub in range(SUB):
        row_start(z, 0, sub)
    for off in range(1, 2 * nx):
        col_copy(off).start()
    col_pass(0).start()
    col_own.start()

    def ring_step(step):
        for sub in range(SUB):
            for way in range(2):
                if step < hops[way]:
                    ring_copy(way, step, sub).wait_recv()
                    block = ring_block(way, step + 1)
                    if step + 1 < hops[way]:
                        ring_copy(way, step + 1, sub).start()
                    row_start(block, step + 1, sub)

    def pag_copy(off):
        other = lax.rem(chip + off, 2 * nx)
        return remote(pbuf.at[r], pbuf.at[r], pag_send.at[off], pag_recv.at[r], dev(2 * other + k, z, yh))

    def pag_wait(source):
        remote(pown, pbuf.at[source], pag_send.at[0], pag_recv.at[source], dev(r, z, yh)).wait_recv()

    def pag_pass(off):
        source = col_from(off)
        return remote(
            pbuf.at[source], pbuf.at[source], pag_send.at[2 * nx + off], pag_recv.at[source], dev(2 * chip + 1 - k, z, yh)
        )

    def sum_start():
        perm.wait_recv()
        for off in range(1, 2 * nx):
            pag_copy(off).start()
        pag_pass(0).start()

    def sum_pass():
        for off in range(1, 2 * nx):
            pag_wait(col_from(off))
            pag_pass(off).start()

    yx_copy = remote(yx_send, yx_recv, yx_sem.at[0], yx_sem.at[1], dev(r, z, 1 - yh))
    yq_copy = remote(yq_send, yq_recv, yx_sem.at[2], yx_sem.at[3], dev(r, z, 1 - yh))

    def sum_partial():
        for off in range(2 * nx):
            pag_wait(2 * lax.rem(chip + off, 2 * nx) + 1 - k)
        total = jnp.zeros((8, 128), F32)
        for source in range(nr):
            held = pbuf[source, 0:own, :].astype(F32)
            pfull[source * own : (source + 1) * own, :] = held
            total = total + pbuf[source, own : own + 8, 0:128].astype(F32)
        yq_send[...] = jnp.sum(total, axis=0, keepdims=True)
        spart[...] = jnp.dot(a_ref[...], pfull[...].astype(BF16), preferred_element_type=F32)
        yx_send[...] = spart[pl.ds(pl.multiple_of((1 - yh) * half, 8), half), :].astype(BF16)
        yx_copy.start()
        yq_copy.start()

    def zs_copy(off):
        to = dev(r, lax.rem(z + off, nz), yh)
        return remote(zs_buf.at[z], zs_buf.at[z], zs_send.at[off], zs_recv.at[z], to)

    def zq_copy(off):
        to = dev(r, lax.rem(z + off, nz), yh)
        return remote(zq_buf.at[z], zq_buf.at[z], zq_send.at[off], zq_recv.at[z], to)

    def sum_across():
        yx_copy.wait_recv()
        yq_copy.wait_recv()
        both = spart[pl.ds(pl.multiple_of(yh * half, 8), half), :] + yx_recv[...].astype(F32)
        zs_buf[z] = both.astype(BF16)
        zq_buf[z] = yq_send[...] + yq_recv[...]
        for off in range(1, nz):
            zs_copy(off).start()
        for off in range(1, nz):
            zq_copy(off).start()

    def pln_copy(off):
        other = lax.rem(plane + off, 2 * nr)
        to = dev(lax.div(other, 2), z, lax.rem(other, 2))
        return remote(s_ref.at[plane], s_ref.at[plane], pln_send.at[off], pln_recv.at[plane], to)

    def sum_total():
        for off in range(1, nz):
            source = lax.rem(z + off, nz)
            remote(zs_buf.at[z], zs_buf.at[source], zs_send.at[0], zs_recv.at[source], dev(r, z, yh)).wait_recv()
            remote(zq_buf.at[z], zq_buf.at[source], zq_send.at[0], zq_recv.at[source], dev(r, z, yh)).wait_recv()
        total = zs_buf[0].astype(F32)
        squares = zq_buf[0]
        for source in range(1, nz):
            total = total + zs_buf[source].astype(F32)
            squares = squares + zq_buf[source]
        s_ref[plane] = total.astype(BF16)
        q_ref[...] = squares
        for off in range(1, 2 * nr):
            pln_copy(off).start()

    after = {2: (sum_start,), 3: (sum_pass, sum_partial), 4: (sum_across,), 6: (sum_total,)}
    last = hops[0] - 1
    for step in range(hops[0]):
        ring_step(step)
        for work in after.get(step, ()) if last == 7 else ():
            work()
    if last != 7:
        for work in (sum_start, sum_pass, sum_partial, sum_across, sum_total):
            work()

    for off in range(1, 2 * nx):
        source = col_from(off)
        col_wait(source)
        col_pass(off).start()
    for off in range(2 * nx):
        col_wait(2 * lax.rem(chip + off, 2 * nx) + 1 - k)
    col_own.wait()
    for source in range(1, 2 * nr):
        other = lax.rem(plane + source, 2 * nr)
        remote(s_ref.at[plane], s_ref.at[other], pln_send.at[0], pln_recv.at[other], dev(r, z, yh)).wait_recv()
    for from_yh in range(2):
        for source in range(nr):
            for sub in range(SUB):
                pltpu.make_async_copy(
                    piece(z, 0, sub), rowp_ref.at[from_yh, source, sub], row_recv.at[from_yh, source, sub]
                ).wait()

    @pl.when(jnp.logical_not(fixed))
    def _():
        perm_out.wait_send()

    for way in range(2):
        for step in range(hops[way]):
            for sub in range(SUB):
                ring_copy(way, step, sub).wait_send()
    for block in range(nr):
        for to_yh in range(2):

            @pl.when(jnp.logical_not((r == block) & (yh == to_yh)))
            def _():
                for sub in range(SUB):
                    row_copy(block, 0, to_yh, sub).wait_send()

    for off in range(1, 2 * nx):
        col_copy(off).wait_send()
        pag_copy(off).wait_send()
    for off in range(2 * nx):
        col_pass(off).wait_send()
        pag_pass(off).wait_send()
    yx_copy.wait_send()
    yq_copy.wait_send()
    for off in range(1, nz):
        zs_copy(off).wait_send()
        zq_copy(off).wait_send()
    for off in range(1, 2 * nr):
        pln_copy(off).wait_send()


def exchange(activations, down_weight, keep_mask):
    nx = lax.axis_size("row_1")
    nz = lax.axis_size("col_0")
    nr = 4 * nx
    rows, width = activations.shape
    own, out = down_weight.shape
    half = rows // 2
    hops = nz // 2
    dma = pltpu.SemaphoreType.DMA
    vmem = pl.BlockSpec(memory_space=pltpu.VMEM)
    hbm = pl.BlockSpec(memory_space=pl.ANY)
    return pl.pallas_call(
        functools.partial(exchange_kernel, nx, nz),
        out_shape=(
            jax.ShapeDtypeStruct((2, nr, SUB, rows // SUB, width), BF16),
            jax.ShapeDtypeStruct((nr, rows, width), BF16),
            jax.ShapeDtypeStruct((2 * nr, half, out), BF16),
            jax.ShapeDtypeStruct((1, 128), F32),
        ),
        in_specs=[vmem] * 3,
        out_specs=(hbm, hbm, vmem, vmem),
        scratch_shapes=[
            pltpu.VMEM((nz, SUB, rows // SUB, width), BF16),
            pltpu.VMEM((own + 8, out), BF16),
            pltpu.VMEM((nr, own + 8, out), BF16),
            pltpu.VMEM((width, out), F32),
            pltpu.VMEM((rows, out), F32),
            pltpu.VMEM((half, out), BF16),
            pltpu.VMEM((half, out), BF16),
            pltpu.VMEM((1, 128), F32),
            pltpu.VMEM((1, 128), F32),
            pltpu.VMEM((nz, half, out), BF16),
            pltpu.VMEM((nz, 1, 128), F32),
            dma((2, hops, SUB)),
            dma((2, hops, SUB)),
            dma((nr, 2, SUB)),
            dma((2, nr, SUB)),
            dma((4 * nx,)),
            dma((nr,)),
            dma((2,)),
            dma((4 * nx,)),
            dma((nr,)),
            dma((4,)),
            dma((nz,)),
            dma((nz,)),
            dma((nz,)),
            dma((nz,)),
            dma((2 * nr,)),
            dma((2 * nr,)),
        ],
        compiler_params=pltpu.CompilerParams(collective_id=0, has_side_effects=True),
        name="exchange",
    )(activations, down_weight, keep_mask)


def local(activations, down_weight, keep_mask):
    row_count = lax.axis_size(ROW)
    col_count = lax.axis_size(COL)
    row_index = lax.axis_index(ROW)
    col_index = lax.axis_index(COL)
    width = activations.shape[1]
    samples = activations.shape[0] * row_count
    own_rows, out = down_weight.shape
    row_panels, col_panel, s, squares = exchange(activations, down_weight, keep_mask)
    row_panels = row_panels.reshape(2, samples, width)
    col_panel = col_panel.reshape(samples, width)
    s = s.reshape(samples, out)
    mean_square = squares[0, 0] / (samples * width * col_count) + 1e-06
    damping = damp_ratio * mean_square
    tiles = []
    for part in range(2):
        tile = lax.dot_general(row_panels[part], col_panel, (((0,), (0,)), ((), ())), preferred_element_type=F32)
        tiles.append(tile / samples)
    gram_tile = jnp.concatenate(tiles, axis=0)
    tile_rows = 2 * width
    global_rows = row_index * tile_rows + lax.iota(jnp.int32, tile_rows)
    global_cols = col_index * width + lax.iota(jnp.int32, width)
    gram_damped = (
        gram_tile + jnp.where(global_rows[:, None] == global_cols[None, :], damping, jnp.float32(0.0))
    ).astype(BF16)
    picked = lax.dynamic_slice(
        row_panels, (col_index // row_count, 0, col_index % row_count * own_rows), (1, samples, own_rows)
    )[0]
    descent = lax.dot_general(picked, s, (((0,), (0,)), ((), ())), preferred_element_type=F32) / samples
    keep_float = keep_mask.astype(F32)
    updated = keep_float * (
        down_weight.astype(F32) + step_ratio * descent / ((1.0 + damp_ratio) * mean_square)
    )
    return gram_damped, updated.astype(BF16)


def solution(mesh):
    torus = Mesh(mesh.devices.reshape(2, 4, 2, 16, 2), AXES)
    in_specs = (P(ROW, COL), P(AXES, None), P(AXES, None))
    out_specs = (P(ROW, COL), P(AXES, None))
    return jax.shard_map(local, mesh=torus, in_specs=in_specs, out_specs=out_specs, check_vma=False)
```

```python
import functools

import jax
import jax.numpy as jnp
from jax import lax
from jax.experimental import pallas as pl
from jax.experimental.pallas import tpu as pltpu
from jax.sharding import Mesh
from jax.sharding import PartitionSpec as P

MESH = pl.DeviceIdType.MESH
AXES = ("row_0", "row_1", "row_2", "col_0", "col_1")
ROW = AXES[:3]
COL = AXES[3:]
F32 = jnp.float32
BF16 = jnp.bfloat16
SUB = 2
NEAR = 4
AFTER = {1: ("weights",), 2: ("partial",), 3: ("columns", "near")}

damp_ratio = 0.1
step_ratio = 0.25


def each(low, high, work):
    def step(i, carry):
        work(i)
        return carry

    lax.fori_loop(low, high, step, 0)


def exchange_kernel(
    nx,
    nz,
    a_ref,
    dw_ref,
    mask_ref,
    rowp_ref,
    colp_ref,
    s_ref,
    q_ref,
    zbuf,
    xbuf,
    abuf,
    pown,
    pbuf,
    pfull,
    spart,
    near_out,
    near_in,
    nearq_out,
    nearq_in,
    far_buf,
    farq_buf,
    ring_send,
    ring_recv,
    x_send,
    x_recv,
    row_send,
    row_recv,
    col_send,
    col_recv,
    perm_sem,
    pair_sem,
    pag_send,
    pag_recv,
    near_send,
    near_recv,
    nearq_send,
    nearq_recv,
    far_send,
    far_recv,
    farq_send,
    farq_recv,
    pln_send,
    pln_recv,
):
    nr = 4 * nx
    chips = 2 * nx
    own = dw_ref.shape[0]
    rows, width = a_ref.shape
    half = rows // 2
    sub_rows = rows // SUB
    yl, x, k, z, yh = (lax.axis_index(name) for name in AXES)
    chip = yl * nx + x
    r = chip * 2 + k
    plane = 2 * r + yh
    ngroup = 4 * NEAR
    nfar = nz // NEAR
    zl, zb = lax.rem(z, NEAR), lax.div(z, NEAR)
    mate = (k * NEAR + zl) * 2 + yh

    def dev(r_, z_, yh_):
        return dict(
            row_0=lax.div(r_, 2 * nx),
            row_1=lax.rem(lax.div(r_, 2), nx),
            row_2=lax.rem(r_, 2),
            col_0=z_,
            col_1=yh_,
        )

    def in_plane(flat):
        return dev(lax.div(flat, 2), z, lax.rem(flat, 2))

    def in_near(flat):
        return dev(2 * chip + lax.div(flat, 2 * NEAR), zb * NEAR + lax.rem(lax.div(flat, 2), NEAR), lax.rem(flat, 2))

    def remote(src, dst, send, recv, to):
        return pltpu.make_async_remote_copy(
            src_ref=src, dst_ref=dst, send_sem=send, recv_sem=recv, device_id=to, device_id_type=MESH
        )

    def arrived(dst, sem):
        pltpu.make_async_copy(dst, dst, sem).wait()

    t_r, t_yh = 2 * lax.rem(z, nz // 2) + yh, lax.div(z, nz // 2)
    target = dev(t_r, r, t_yh)
    source = dev(z, yh * (nz // 2) + lax.div(r, 2), lax.rem(r, 2))
    fixed = (t_r == r) & (r == z) & (t_yh == yh)

    barrier = pltpu.get_barrier_semaphore()

    def greet(to):
        pl.semaphore_signal(barrier, inc=1, device_id=to, device_id_type=MESH)

    greet(target)
    greet(source)
    greeted = 2
    each(1, nfar, lambda off: greet(dev(r, lax.rem(z + off * NEAR, nz), yh)))
    greeted += nfar - 1
    for off in (1, 2, nz - 2, nz - 1):
        greet(dev(r, lax.rem(z + off, nz), yh))
        greeted += 1
    for core in range(2):
        for to_yh in range(2):
            each(1, NEAR, lambda off: greet(dev(2 * chip + core, zb * NEAR + lax.rem(zl + off, NEAR), to_yh)))
            greeted += NEAR - 1
    each(1, 2 * nr, lambda off: greet(in_plane(lax.rem(plane + off, 2 * nr))))
    greeted += 2 * nr - 1

    pown[0:own, :] = dw_ref[...] * (1 - mask_ref[...]).astype(BF16)
    act = a_ref[...].astype(F32)
    square = jnp.sum(jnp.sum(act * act, axis=0, keepdims=True), axis=1, keepdims=True)
    square = jnp.broadcast_to(square, (8, 256))
    high = square.astype(BF16).astype(F32)
    middle = (square - high).astype(BF16).astype(F32)
    low = (square - high - middle).astype(BF16).astype(F32)
    line = lax.broadcasted_iota(jnp.int32, (8, 256), 0)
    zero = jnp.zeros((8, 256), F32)
    coded = jnp.where(line == 0, high, jnp.where(line == 1, middle, jnp.where(line == 2, low, zero)))
    pown[own : own + 8, :] = coded.astype(BF16)
    pfull[...] = jnp.zeros(pfull.shape, F32)

    pl.semaphore_wait(barrier, greeted)

    perm = remote(pown, pbuf.at[t_r], perm_sem.at[0], perm_sem.at[1], target)
    perm_here = pltpu.make_async_copy(pown, pbuf.at[r], perm_sem.at[1])

    @pl.when(jnp.logical_not(fixed))
    def _():
        perm.start()

    @pl.when(fixed)
    def _():
        perm_here.start()

    reach = (nz // 2, nz - 1 - nz // 2)

    def block_at(way, dist):
        return lax.rem(z + nz - dist, nz) if way == 0 else lax.rem(z + dist, nz)

    def piece(block, dist, sub):
        if dist == 0:
            return a_ref.at[pl.ds(pl.multiple_of(sub * sub_rows, sub_rows), sub_rows)]
        return zbuf.at[block, sub]

    def ring_copy(way, dist, sub):
        hop = 1 if dist % 2 else 2
        block = block_at(way, dist - hop)
        to = lax.rem(z + hop, nz) if way == 0 else lax.rem(z + nz - hop, nz)
        return remote(
            piece(block, dist - hop, sub),
            zbuf.at[block, sub],
            ring_send.at[way, dist - 1, sub],
            ring_recv.at[way, dist - 1, sub],
            dev(r, to, yh),
        )

    def ring_from(way, dist, sub):
        for further in (dist + 2, dist + 1):
            if further <= reach[way]:
                ring_copy(way, further, sub).start()

    def column(block):
        return lax.rem(lax.div(block, 2), nx)

    def place(block):
        return lax.div(block, 2 * nx) * 2 + lax.rem(block, 2)

    def row_copy(block, xs, sub, src, to_yh):
        rs = (yl * nx + xs) * 2 + k
        return remote(
            src,
            rowp_ref.at[yh, rs, sub],
            row_send.at[place(block), xs, to_yh, sub],
            row_recv.at[yh, rs, sub],
            dev(block, z, to_yh),
        )

    def deliver(block, xs, sub, src):
        def one(to_yh):
            here = (block == r) & (yh == to_yh)

            @pl.when(jnp.logical_not(here))
            def _():
                row_copy(block, xs, sub, src, to_yh).start()

            @pl.when(here)
            def _():
                rs = (yl * nx + xs) * 2 + k
                pltpu.make_async_copy(src, rowp_ref.at[yh, rs, sub], row_recv.at[yh, rs, sub]).start()

        each(0, 2, one)

    def x_copy(block, dist, sub):
        return remote(
            piece(block, dist, sub),
            xbuf.at[place(block), x, sub],
            x_send.at[block, sub],
            x_recv.at[place(block), x, sub],
            dev((yl * nx + column(block)) * 2 + k, z, yh),
        )

    def spread(block, dist, sub):
        @pl.when(column(block) == x)
        def _():
            deliver(block, x, sub, piece(block, dist, sub))

        @pl.when(column(block) != x)
        def _():
            x_copy(block, dist, sub).start()

    def relay(block, sub):
        @pl.when(column(block) == x)
        def _():
            def one(off):
                xs = lax.rem(x + off, nx)
                held = xbuf.at[place(block), xs, sub]
                arrived(held, x_recv.at[place(block), xs, sub])
                deliver(block, xs, sub, held)

            each(1, nx, one)

    def col_copy(off):
        other = lax.rem(chip + off, chips)
        return remote(a_ref, colp_ref.at[r], col_send.at[off], col_recv.at[r], dev(2 * other + k, z, yh))

    def col_from(off):
        return 2 * lax.rem(chip + chips - off, chips) + k

    pair = dev(2 * chip + 1 - k, z, yh)

    def col_pass(off, src):
        rs = col_from(off)
        return remote(src, colp_ref.at[rs], col_send.at[chips + off], col_recv.at[rs], pair)

    col_own = pltpu.make_async_copy(a_ref, colp_ref.at[r], col_recv.at[r])
    pair_copy = remote(a_ref, abuf, pair_sem.at[0], pair_sem.at[1], pair)

    for sub in range(SUB):
        for way in range(2):
            ring_from(way, 0, sub)
    for sub in range(SUB):
        spread(z, 0, sub)
    pair_copy.start()
    each(1, chips, lambda off: col_copy(off).start())
    col_pass(0, a_ref).start()
    col_own.start()

    def ring_round(t):
        near, far = 2 * t + 1, 2 * t + 2
        for dist in (far, near):

            def one(sub):
                for way in range(2):
                    if dist <= reach[way]:
                        block = block_at(way, dist)
                        arrived(zbuf.at[block, sub], ring_recv.at[way, dist - 1, sub])
                        if dist == far:
                            ring_from(way, dist, sub)
                        spread(block, dist, sub)

            each(0, SUB, one)

    def relay_round(t):
        for dist in (2 * t, 2 * t - 1) if t else (0,):

            def one(sub):
                for way in range(2 if t else 1):
                    if dist <= reach[way]:
                        relay(block_at(way, dist), sub)

            each(0, SUB, one)

    def pag_copy(off):
        other = lax.rem(chip + off, chips)
        return remote(pbuf.at[r], pbuf.at[r], pag_send.at[off], pag_recv.at[r], dev(2 * other + k, z, yh))

    def weights():
        arrived(pbuf.at[r], perm_sem.at[1])
        each(1, chips, lambda off: pag_copy(off).start())

    def near_copy(off):
        to = lax.rem(mate + off, ngroup)
        src = near_out.at[lax.div(to, 2 * NEAR), lax.rem(to, 2)]
        return remote(src, near_in.at[mate], near_send.at[off], near_recv.at[mate], in_near(to))

    def nearq_copy(off):
        to = in_near(lax.rem(mate + off, ngroup))
        return remote(nearq_out, nearq_in.at[mate], nearq_send.at[off], nearq_recv.at[mate], to)

    def partial():
        total = pbuf[r, own : own + 8, 0:128].astype(F32)
        pfull[pl.ds(pl.multiple_of(r * own, 8), own), :] = pbuf[r, 0:own, :].astype(F32)
        for off in range(1, chips):
            rs = col_from(off)
            arrived(pbuf.at[rs], pag_recv.at[rs])
            pfull[pl.ds(pl.multiple_of(rs * own, 8), own), :] = pbuf[rs, 0:own, :].astype(F32)
            total = total + pbuf[rs, own : own + 8, 0:128].astype(F32)
        arrived(abuf, pair_sem.at[1])
        weight = pfull[...].astype(BF16)
        mine = jnp.dot(a_ref[...], weight, preferred_element_type=F32)
        other = jnp.dot(abuf[...], weight, preferred_element_type=F32)
        spart[...] = mine
        for to_yh in range(2):
            near_out[k, to_yh] = mine[to_yh * half : (to_yh + 1) * half].astype(BF16)
            near_out[1 - k, to_yh] = other[to_yh * half : (to_yh + 1) * half].astype(BF16)
        nearq_out[...] = jnp.sum(total, axis=0, keepdims=True)
        each(1, ngroup, lambda off: near_copy(off).start())
        each(1, ngroup, lambda off: nearq_copy(off).start())

    def far_copy(off):
        to = dev(r, lax.rem(z + off * NEAR, nz), yh)
        return remote(far_buf.at[zb], far_buf.at[zb], far_send.at[off], far_recv.at[zb], to)

    def farq_copy(off):
        to = dev(r, lax.rem(z + off * NEAR, nz), yh)
        return remote(farq_buf.at[zb], farq_buf.at[zb], farq_send.at[off], farq_recv.at[zb], to)

    def near():
        total = spart[pl.ds(pl.multiple_of(yh * half, 8), half), :]
        squares = nearq_out[...]
        for off in range(1, ngroup):
            other = lax.rem(mate + off, ngroup)
            arrived(near_in.at[other], near_recv.at[other])
            total = total + near_in[other].astype(F32)
        for off in range(1, ngroup):
            other = lax.rem(mate + off, ngroup)
            arrived(nearq_in.at[other], nearq_recv.at[other])
            squares = squares + nearq_in[other]
        far_buf[zb] = total.astype(BF16)
        farq_buf[zb] = squares
        for off in range(1, nfar):
            far_copy(off).start()
            farq_copy(off).start()

    def pln_copy(off):
        to = in_plane(lax.rem(plane + off, 2 * nr))
        return remote(s_ref.at[plane], s_ref.at[plane], pln_send.at[off], pln_recv.at[plane], to)

    def far():
        for off in range(1, nfar):
            other = lax.rem(zb + off, nfar)
            arrived(far_buf.at[other], far_recv.at[other])
            arrived(farq_buf.at[other], farq_recv.at[other])
        total = far_buf[0].astype(F32)
        squares = farq_buf[0]
        for other in range(1, nfar):
            total = total + far_buf[other].astype(F32)
            squares = squares + farq_buf[other]
        s_ref[plane] = total.astype(BF16)
        q_ref[...] = squares
        each(1, 2 * nr, lambda off: pln_copy(off).start())

    def columns():
        def one(off):
            rs = col_from(off)
            arrived(colp_ref.at[rs], col_recv.at[rs])
            col_pass(off, colp_ref.at[rs]).start()

        each(1, chips, one)

    stages = dict(weights=weights, partial=partial, near=near, far=far, columns=columns)
    done = []
    rounds = (reach[0] + 1) // 2
    for t in range(rounds):
        ring_round(t)
        relay_round(t)
        for name in AFTER.get(t, ()):
            stages[name]()
            done.append(name)
    relay_round(rounds)
    for name in ("weights", "partial", "columns", "near", "far"):
        if name not in done:
            stages[name]()

    def wait_col(off):
        rs = 2 * lax.rem(chip + off, chips) + 1 - k
        arrived(colp_ref.at[rs], col_recv.at[rs])

    def wait_plane(off):
        other = lax.rem(plane + off, 2 * nr)
        arrived(s_ref.at[other], pln_recv.at[other])

    def wait_row(i):
        from_yh, rs = lax.div(i, nr), lax.rem(i, nr)
        for sub in range(SUB):
            arrived(rowp_ref.at[from_yh, rs, sub], row_recv.at[from_yh, rs, sub])

    each(0, chips, wait_col)
    col_own.wait()
    each(0, 2 * nr, wait_row)
    each(1, 2 * nr, wait_plane)

    @pl.when(jnp.logical_not(fixed))
    def _():
        perm.wait_send()

    def wait_ring(sub):
        for way in range(2):
            for dist in range(1, reach[way] + 1):
                ring_copy(way, dist, sub).wait_send()

    each(0, SUB, wait_ring)

    def wait_block(block):
        @pl.when(column(block) != x)
        def _():
            for sub in range(SUB):
                x_copy(block, 0, sub).wait_send()

        @pl.when(column(block) == x)
        def _():
            def one(i):
                xs, to_yh = lax.div(i, 2), lax.rem(i, 2)

                @pl.when(jnp.logical_not((r == block) & (yh == to_yh)))
                def _():
                    for sub in range(SUB):
                        row_copy(block, xs, sub, piece(block, 0, sub), to_yh).wait_send()

            each(0, 2 * nx, one)

    each(0, nz, wait_block)

    def wait_chip(off):
        col_copy(off).wait_send()
        pag_copy(off).wait_send()

    def wait_near(off):
        near_copy(off).wait_send()
        nearq_copy(off).wait_send()

    def wait_far(off):
        far_copy(off).wait_send()
        farq_copy(off).wait_send()

    pair_copy.wait_send()
    each(1, chips, wait_chip)
    each(0, chips, lambda off: arrived(a_ref, col_send.at[chips + off]))
    each(1, ngroup, wait_near)
    each(1, nfar, wait_far)
    each(1, 2 * nr, lambda off: pln_copy(off).wait_send())


def exchange(activations, down_weight, keep_mask):
    nx = lax.axis_size("row_1")
    nz = lax.axis_size("col_0")
    nr = 4 * nx
    chips = 2 * nx
    rows, width = activations.shape
    own, out = down_weight.shape
    half = rows // 2
    sub_rows = rows // SUB
    reach = nz // 2
    ngroup = 4 * NEAR
    nfar = nz // NEAR
    dma = pltpu.SemaphoreType.DMA
    vmem = pl.BlockSpec(memory_space=pltpu.VMEM)
    hbm = pl.BlockSpec(memory_space=pl.ANY)
    return pl.pallas_call(
        functools.partial(exchange_kernel, nx, nz),
        out_shape=(
            jax.ShapeDtypeStruct((2, nr, SUB, sub_rows, width), BF16),
            jax.ShapeDtypeStruct((nr, rows, width), BF16),
            jax.ShapeDtypeStruct((2 * nr, half, out), BF16),
            jax.ShapeDtypeStruct((1, 128), F32),
        ),
        in_specs=[vmem] * 3,
        out_specs=(hbm, hbm, vmem, vmem),
        scratch_shapes=[
            pltpu.VMEM((nz, SUB, sub_rows, width), BF16),
            pltpu.VMEM((4, nx, SUB, sub_rows, width), BF16),
            pltpu.VMEM((rows, width), BF16),
            pltpu.VMEM((own + 8, out), BF16),
            pltpu.VMEM((nr, own + 8, out), BF16),
            pltpu.VMEM((width, out), F32),
            pltpu.VMEM((rows, out), F32),
            pltpu.VMEM((2, 2, half, out), BF16),
            pltpu.VMEM((ngroup, half, out), BF16),
            pltpu.VMEM((1, 128), F32),
            pltpu.VMEM((ngroup, 1, 128), F32),
            pltpu.VMEM((nfar, half, out), BF16),
            pltpu.VMEM((nfar, 1, 128), F32),
            dma((2, reach, SUB)),
            dma((2, reach, SUB)),
            dma((nz, SUB)),
            dma((4, nx, SUB)),
            dma((4, nx, 2, SUB)),
            dma((2, nr, SUB)),
            dma((2 * chips,)),
            dma((nr,)),
            dma((2,)),
            dma((2,)),
            dma((chips,)),
            dma((nr,)),
            dma((ngroup,)),
            dma((ngroup,)),
            dma((ngroup,)),
            dma((ngroup,)),
            dma((nfar,)),
            dma((nfar,)),
            dma((nfar,)),
            dma((nfar,)),
            dma((2 * nr,)),
            dma((2 * nr,)),
        ],
        compiler_params=pltpu.CompilerParams(collective_id=0, has_side_effects=True),
        name="exchange",
    )(activations, down_weight, keep_mask)


def products_kernel(samples, count, row_ref, col_ref, s_ref, q_ref, dw_ref, mask_ref, gram_ref, upd_ref, drop):
    part = pl.program_id(0)
    width = col_ref.shape[1]
    own = dw_ref.shape[0]
    row_count = lax.axis_size(ROW)
    r, c = lax.axis_index(ROW), lax.axis_index(COL)
    mean_square = q_ref[...] / count + 1e-06
    damping = jnp.where(2 * r + part == c, 1.0, 0.0) * (damp_ratio * mean_square)
    eye = lax.broadcasted_iota(jnp.int32, (128, 128), 0) == lax.broadcasted_iota(jnp.int32, (128, 128), 1)
    extra = jnp.where(eye, jnp.broadcast_to(damping, (128, 128)), 0.0)
    over_rows = (((0,), (0,)), ((), ()))
    for tile in range(width // 128):
        low = tile * 128
        gram = lax.dot_general(row_ref[0, :, low : low + 128], col_ref[...], over_rows, preferred_element_type=F32)
        gram = gram / samples
        gram_ref[low : low + 128, :] = gram.astype(BF16)
        gram_ref[low : low + 128, low : low + 128] = (gram[:, low : low + 128] + extra).astype(BF16)

    first = lax.rem(c, row_count) * own

    @pl.when(part == lax.div(c, row_count))
    def _():
        low = jnp.minimum(lax.div(first, 128) * 128, width - 256)
        window = row_ref[0, :, pl.ds(pl.multiple_of(low, 128), 256)]
        drop[...] = lax.dot_general(window, s_ref[...], over_rows, preferred_element_type=F32) / samples
        descent = drop[pl.ds(pl.multiple_of(first - low, 8), own), :]
        scale = jnp.broadcast_to((1.0 + damp_ratio) * mean_square[:, 0:1], descent.shape)
        updated = dw_ref[...].astype(F32) + step_ratio * descent / scale
        upd_ref[...] = (mask_ref[...].astype(F32) * updated).astype(BF16)


def products(row_panels, col_panel, s, squares, down_weight, keep_mask, count):
    _, samples, width = row_panels.shape
    own, out = down_weight.shape

    def whole(shape):
        return pl.BlockSpec(shape, lambda part: (0,) * len(shape))

    return pl.pallas_call(
        functools.partial(products_kernel, samples, count),
        out_shape=(jax.ShapeDtypeStruct((2 * width, width), BF16), jax.ShapeDtypeStruct((own, out), BF16)),
        grid=(2,),
        in_specs=[
            pl.BlockSpec((1, samples, width), lambda part: (part, 0, 0)),
            whole(col_panel.shape),
            whole(s.shape),
            whole(squares.shape),
            whole(down_weight.shape),
            whole(keep_mask.shape),
        ],
        out_specs=(pl.BlockSpec((width, width), lambda part: (part, 0)), whole((own, out))),
        scratch_shapes=[pltpu.VMEM((256, out), F32)],
        name="products",
    )(row_panels, col_panel, s, squares, down_weight, keep_mask)


def local(activations, down_weight, keep_mask):
    rows, width = activations.shape
    samples = rows * lax.axis_size(ROW)
    out = down_weight.shape[1]
    row_panels, col_panel, s, squares = exchange(activations, down_weight, keep_mask)
    return products(
        row_panels.reshape(2, samples, width),
        col_panel.reshape(samples, width),
        s.reshape(samples, out),
        squares,
        down_weight,
        keep_mask,
        samples * width * lax.axis_size(COL),
    )


def solution(mesh):
    torus = Mesh(mesh.devices.reshape(2, 4, 2, 16, 2), AXES)
    in_specs = (P(ROW, COL), P(AXES, None), P(AXES, None))
    out_specs = (P(ROW, COL), P(AXES, None))
    return jax.shard_map(local, mesh=torus, in_specs=in_specs, out_specs=out_specs, check_vma=False)
```

```python
import functools

import jax
import jax.numpy as jnp
from jax import lax
from jax.experimental import pallas as pl
from jax.experimental.pallas import tpu as pltpu
from jax.sharding import Mesh
from jax.sharding import PartitionSpec as P

MESH = pl.DeviceIdType.MESH
AXES = ("row_0", "row_1", "row_2", "col_0", "col_1")
ROW = AXES[:3]
COL = AXES[3:]
F32 = jnp.float32
BF16 = jnp.bfloat16
SUB = 1
NEAR = 4
AFTER = {1: ("weights",), 2: ("partial",)}
LATER = {3: ("near", "columns")}

damp_ratio = 0.1
step_ratio = 0.25


def each(low, high, work):
    def step(i, carry):
        work(i)
        return carry

    lax.fori_loop(low, high, step, 0)


def exchange_kernel(
    nx,
    nz,
    a_ref,
    dw_ref,
    mask_ref,
    rowp_ref,
    colp_ref,
    s_ref,
    q_ref,
    zbuf,
    xbuf,
    abuf,
    pown,
    pbuf,
    pfull,
    spart,
    near_out,
    near_in,
    nearq_out,
    nearq_in,
    far_buf,
    farq_buf,
    ring_send,
    ring_recv,
    x_send,
    x_recv,
    row_send,
    row_recv,
    col_send,
    col_recv,
    perm_sem,
    pair_sem,
    pag_send,
    pag_recv,
    near_send,
    near_recv,
    nearq_send,
    nearq_recv,
    far_send,
    far_recv,
    farq_send,
    farq_recv,
    pln_send,
    pln_recv,
):
    nr = 4 * nx
    chips = 2 * nx
    own = dw_ref.shape[0]
    rows, width = a_ref.shape
    half = rows // 2
    sub_rows = rows // SUB
    yl, x, k, z, yh = (lax.axis_index(name) for name in AXES)
    chip = yl * nx + x
    r = chip * 2 + k
    plane = 2 * r + yh
    ngroup = 4 * NEAR
    nfar = nz // NEAR
    zl, zb = lax.rem(z, NEAR), lax.div(z, NEAR)
    mate = (k * NEAR + zl) * 2 + yh

    def dev(r_, z_, yh_):
        return dict(
            row_0=lax.div(r_, 2 * nx),
            row_1=lax.rem(lax.div(r_, 2), nx),
            row_2=lax.rem(r_, 2),
            col_0=z_,
            col_1=yh_,
        )

    def in_plane(flat):
        return dev(lax.div(flat, 2), z, lax.rem(flat, 2))

    def in_near(flat):
        return dev(2 * chip + lax.div(flat, 2 * NEAR), zb * NEAR + lax.rem(lax.div(flat, 2), NEAR), lax.rem(flat, 2))

    def remote(src, dst, send, recv, to):
        return pltpu.make_async_remote_copy(
            src_ref=src, dst_ref=dst, send_sem=send, recv_sem=recv, device_id=to, device_id_type=MESH
        )

    def arrived(dst, sem):
        pltpu.make_async_copy(dst, dst, sem).wait()

    t_r, t_yh = 2 * lax.rem(z, nz // 2) + yh, lax.div(z, nz // 2)
    target = dev(t_r, r, t_yh)
    source = dev(z, yh * (nz // 2) + lax.div(r, 2), lax.rem(r, 2))
    fixed = (t_r == r) & (r == z) & (t_yh == yh)

    barrier = pltpu.get_barrier_semaphore()

    def greet(to):
        pl.semaphore_signal(barrier, inc=1, device_id=to, device_id_type=MESH)

    greet(target)
    greet(source)
    greeted = 2
    each(1, nfar, lambda off: greet(dev(r, lax.rem(z + off * NEAR, nz), yh)))
    greeted += nfar - 1
    for off in (1, 2, nz - 2, nz - 1):
        greet(dev(r, lax.rem(z + off, nz), yh))
        greeted += 1
    for core in range(2):
        for to_yh in range(2):
            each(1, NEAR, lambda off: greet(dev(2 * chip + core, zb * NEAR + lax.rem(zl + off, NEAR), to_yh)))
            greeted += NEAR - 1
    each(1, 2 * nr, lambda off: greet(in_plane(lax.rem(plane + off, 2 * nr))))
    greeted += 2 * nr - 1

    pown[0:own, :] = dw_ref[...] * (1 - mask_ref[...]).astype(BF16)
    act = a_ref[...].astype(F32)
    square = jnp.sum(jnp.sum(act * act, axis=0, keepdims=True), axis=1, keepdims=True)
    square = jnp.broadcast_to(square, (8, 256))
    high = square.astype(BF16).astype(F32)
    middle = (square - high).astype(BF16).astype(F32)
    low = (square - high - middle).astype(BF16).astype(F32)
    line = lax.broadcasted_iota(jnp.int32, (8, 256), 0)
    zero = jnp.zeros((8, 256), F32)
    coded = jnp.where(line == 0, high, jnp.where(line == 1, middle, jnp.where(line == 2, low, zero)))
    pown[own : own + 8, :] = coded.astype(BF16)
    pfull[...] = jnp.zeros(pfull.shape, F32)

    pl.semaphore_wait(barrier, greeted)

    perm = remote(pown, pbuf.at[t_r], perm_sem.at[0], perm_sem.at[1], target)
    perm_here = pltpu.make_async_copy(pown, pbuf.at[r], perm_sem.at[1])

    @pl.when(jnp.logical_not(fixed))
    def _():
        perm.start()

    @pl.when(fixed)
    def _():
        perm_here.start()

    reach = (nz // 2, nz - 1 - nz // 2)

    def block_at(way, dist):
        return lax.rem(z + nz - dist, nz) if way == 0 else lax.rem(z + dist, nz)

    def piece(block, dist, sub):
        if dist == 0:
            return a_ref.at[pl.ds(pl.multiple_of(sub * sub_rows, sub_rows), sub_rows)]
        return zbuf.at[block, sub]

    def ring_copy(way, dist, sub):
        hop = 1 if dist % 2 else 2
        block = block_at(way, dist - hop)
        to = lax.rem(z + hop, nz) if way == 0 else lax.rem(z + nz - hop, nz)
        return remote(
            piece(block, dist - hop, sub),
            zbuf.at[block, sub],
            ring_send.at[way, dist - 1, sub],
            ring_recv.at[way, dist - 1, sub],
            dev(r, to, yh),
        )

    def ring_from(way, dist, sub):
        for further in (dist + 2, dist + 1):
            if further <= reach[way]:
                ring_copy(way, further, sub).start()

    def column(block):
        return lax.rem(lax.div(block, 2), nx)

    def place(block):
        return lax.div(block, 2 * nx) * 2 + lax.rem(block, 2)

    def row_copy(block, xs, sub, src, to_yh):
        rs = (yl * nx + xs) * 2 + k
        return remote(
            src,
            rowp_ref.at[yh, rs, sub],
            row_send.at[place(block), xs, to_yh, sub],
            row_recv.at[yh, rs, sub],
            dev(block, z, to_yh),
        )

    def deliver(block, xs, sub, src):
        def one(to_yh):
            here = (block == r) & (yh == to_yh)

            @pl.when(jnp.logical_not(here))
            def _():
                row_copy(block, xs, sub, src, to_yh).start()

            @pl.when(here)
            def _():
                rs = (yl * nx + xs) * 2 + k
                pltpu.make_async_copy(src, rowp_ref.at[yh, rs, sub], row_recv.at[yh, rs, sub]).start()

        each(0, 2, one)

    def x_copy(block, dist, sub):
        return remote(
            piece(block, dist, sub),
            xbuf.at[place(block), x, sub],
            x_send.at[block, sub],
            x_recv.at[place(block), x, sub],
            dev((yl * nx + column(block)) * 2 + k, z, yh),
        )

    def spread(block, dist, sub):
        @pl.when(column(block) == x)
        def _():
            deliver(block, x, sub, piece(block, dist, sub))

        @pl.when(column(block) != x)
        def _():
            x_copy(block, dist, sub).start()

    def relay(block, sub):
        @pl.when(column(block) == x)
        def _():
            def one(off):
                xs = lax.rem(x + off, nx)
                held = xbuf.at[place(block), xs, sub]
                arrived(held, x_recv.at[place(block), xs, sub])
                deliver(block, xs, sub, held)

            each(1, nx, one)

    def col_copy(off):
        other = lax.rem(chip + off, chips)
        return remote(a_ref, colp_ref.at[r], col_send.at[off], col_recv.at[r], dev(2 * other + k, z, yh))

    def col_from(off):
        return 2 * lax.rem(chip + chips - off, chips) + k

    pair = dev(2 * chip + 1 - k, z, yh)

    def col_pass(off, src):
        rs = col_from(off)
        return remote(src, colp_ref.at[rs], col_send.at[chips + off], col_recv.at[rs], pair)

    col_own = pltpu.make_async_copy(a_ref, colp_ref.at[r], col_recv.at[r])
    pair_copy = remote(a_ref, abuf, pair_sem.at[0], pair_sem.at[1], pair)

    for sub in range(SUB):
        for way in range(2):
            ring_from(way, 0, sub)
    for sub in range(SUB):
        spread(z, 0, sub)
    pair_copy.start()
    each(1, chips, lambda off: col_copy(off).start())
    col_pass(0, a_ref).start()
    col_own.start()

    def ring_round(t):
        near, far = 2 * t + 1, 2 * t + 2
        for dist in (far, near):

            def one(sub):
                for way in range(2):
                    if dist <= reach[way]:
                        block = block_at(way, dist)
                        arrived(zbuf.at[block, sub], ring_recv.at[way, dist - 1, sub])
                        if dist == far:
                            ring_from(way, dist, sub)

            each(0, SUB, one)

    def spread_round(t):
        def one(sub):
            for dist in (2 * t + 2, 2 * t + 1):
                for way in range(2):
                    if dist <= reach[way]:
                        spread(block_at(way, dist), dist, sub)

        each(0, SUB, one)

    def relay_round(t):
        for dist in (2 * t, 2 * t - 1) if t else (0,):

            def one(sub):
                for way in range(2 if t else 1):
                    if dist <= reach[way]:
                        relay(block_at(way, dist), sub)

            each(0, SUB, one)

    def pag_copy(off):
        other = lax.rem(chip + off, chips)
        return remote(pbuf.at[r], pbuf.at[r], pag_send.at[off], pag_recv.at[r], dev(2 * other + k, z, yh))

    def weights():
        arrived(pbuf.at[r], perm_sem.at[1])
        each(1, chips, lambda off: pag_copy(off).start())

    def near_copy(off):
        to = lax.rem(mate + off, ngroup)
        src = near_out.at[lax.div(to, 2 * NEAR), lax.rem(to, 2)]
        return remote(src, near_in.at[mate], near_send.at[off], near_recv.at[mate], in_near(to))

    def nearq_copy(off):
        to = in_near(lax.rem(mate + off, ngroup))
        return remote(nearq_out, nearq_in.at[mate], nearq_send.at[off], nearq_recv.at[mate], to)

    def partial():
        total = pbuf[r, own : own + 8, 0:128].astype(F32)
        pfull[pl.ds(pl.multiple_of(r * own, 8), own), :] = pbuf[r, 0:own, :].astype(F32)
        for off in range(1, chips):
            rs = col_from(off)
            arrived(pbuf.at[rs], pag_recv.at[rs])
            pfull[pl.ds(pl.multiple_of(rs * own, 8), own), :] = pbuf[rs, 0:own, :].astype(F32)
            total = total + pbuf[rs, own : own + 8, 0:128].astype(F32)
        arrived(abuf, pair_sem.at[1])
        weight = pfull[...].astype(BF16)
        mine = jnp.dot(a_ref[...], weight, preferred_element_type=F32)
        other = jnp.dot(abuf[...], weight, preferred_element_type=F32)
        spart[...] = mine
        for to_yh in range(2):
            near_out[k, to_yh] = mine[to_yh * half : (to_yh + 1) * half].astype(BF16)
            near_out[1 - k, to_yh] = other[to_yh * half : (to_yh + 1) * half].astype(BF16)
        nearq_out[...] = jnp.sum(total, axis=0, keepdims=True)
        each(1, ngroup, lambda off: near_copy(off).start())
        each(1, ngroup, lambda off: nearq_copy(off).start())

    def far_copy(off):
        to = dev(r, lax.rem(z + off * NEAR, nz), yh)
        return remote(far_buf.at[zb], far_buf.at[zb], far_send.at[off], far_recv.at[zb], to)

    def farq_copy(off):
        to = dev(r, lax.rem(z + off * NEAR, nz), yh)
        return remote(farq_buf.at[zb], farq_buf.at[zb], farq_send.at[off], farq_recv.at[zb], to)

    def near():
        total = spart[pl.ds(pl.multiple_of(yh * half, 8), half), :]
        squares = nearq_out[...]
        for off in range(1, ngroup):
            other = lax.rem(mate + off, ngroup)
            arrived(near_in.at[other], near_recv.at[other])
            total = total + near_in[other].astype(F32)
        for off in range(1, ngroup):
            other = lax.rem(mate + off, ngroup)
            arrived(nearq_in.at[other], nearq_recv.at[other])
            squares = squares + nearq_in[other]
        far_buf[zb] = total.astype(BF16)
        farq_buf[zb] = squares
        for off in range(1, nfar):
            far_copy(off).start()
            farq_copy(off).start()

    def pln_copy(off):
        to = in_plane(lax.rem(plane + off, 2 * nr))
        return remote(s_ref.at[plane], s_ref.at[plane], pln_send.at[off], pln_recv.at[plane], to)

    def far():
        for off in range(1, nfar):
            other = lax.rem(zb + off, nfar)
            arrived(far_buf.at[other], far_recv.at[other])
            arrived(farq_buf.at[other], farq_recv.at[other])
        total = far_buf[0].astype(F32)
        squares = farq_buf[0]
        for other in range(1, nfar):
            total = total + far_buf[other].astype(F32)
            squares = squares + farq_buf[other]
        s_ref[plane] = total.astype(BF16)
        q_ref[...] = squares
        each(1, 2 * nr, lambda off: pln_copy(off).start())

    def columns():
        def one(off):
            rs = col_from(off)
            arrived(colp_ref.at[rs], col_recv.at[rs])
            col_pass(off, colp_ref.at[rs]).start()

        each(1, chips, one)

    stages = dict(weights=weights, partial=partial, near=near, far=far, columns=columns)
    done = []
    rounds = (reach[0] + 1) // 2
    for t in range(rounds):
        ring_round(t)
        for name in AFTER.get(t, ()):
            stages[name]()
            done.append(name)
        spread_round(t)
        relay_round(t)
        for name in LATER.get(t, ()):
            stages[name]()
            done.append(name)
    relay_round(rounds)
    for name in ("weights", "partial", "columns", "near", "far"):
        if name not in done:
            stages[name]()

    def wait_col(off):
        rs = 2 * lax.rem(chip + off, chips) + 1 - k
        arrived(colp_ref.at[rs], col_recv.at[rs])

    def wait_plane(off):
        other = lax.rem(plane + off, 2 * nr)
        arrived(s_ref.at[other], pln_recv.at[other])

    def wait_row(i):
        from_yh, rs = lax.div(i, nr), lax.rem(i, nr)
        for sub in range(SUB):
            arrived(rowp_ref.at[from_yh, rs, sub], row_recv.at[from_yh, rs, sub])

    each(0, chips, wait_col)
    col_own.wait()
    each(0, 2 * nr, wait_row)
    each(1, 2 * nr, wait_plane)

    @pl.when(jnp.logical_not(fixed))
    def _():
        perm.wait_send()

    def wait_ring(sub):
        for way in range(2):
            for dist in range(1, reach[way] + 1):
                ring_copy(way, dist, sub).wait_send()

    each(0, SUB, wait_ring)

    def wait_block(block):
        @pl.when(column(block) != x)
        def _():
            for sub in range(SUB):
                x_copy(block, 0, sub).wait_send()

        @pl.when(column(block) == x)
        def _():
            def one(i):
                xs, to_yh = lax.div(i, 2), lax.rem(i, 2)

                @pl.when(jnp.logical_not((r == block) & (yh == to_yh)))
                def _():
                    for sub in range(SUB):
                        row_copy(block, xs, sub, piece(block, 0, sub), to_yh).wait_send()

            each(0, 2 * nx, one)

    each(0, nz, wait_block)

    def wait_chip(off):
        col_copy(off).wait_send()
        pag_copy(off).wait_send()

    def wait_near(off):
        near_copy(off).wait_send()
        nearq_copy(off).wait_send()

    def wait_far(off):
        far_copy(off).wait_send()
        farq_copy(off).wait_send()

    pair_copy.wait_send()
    each(1, chips, wait_chip)
    each(0, chips, lambda off: arrived(a_ref, col_send.at[chips + off]))
    each(1, ngroup, wait_near)
    each(1, nfar, wait_far)
    each(1, 2 * nr, lambda off: pln_copy(off).wait_send())


def exchange(activations, down_weight, keep_mask):
    nx = lax.axis_size("row_1")
    nz = lax.axis_size("col_0")
    nr = 4 * nx
    chips = 2 * nx
    rows, width = activations.shape
    own, out = down_weight.shape
    half = rows // 2
    sub_rows = rows // SUB
    reach = nz // 2
    ngroup = 4 * NEAR
    nfar = nz // NEAR
    dma = pltpu.SemaphoreType.DMA
    vmem = pl.BlockSpec(memory_space=pltpu.VMEM)
    hbm = pl.BlockSpec(memory_space=pl.ANY)
    return pl.pallas_call(
        functools.partial(exchange_kernel, nx, nz),
        out_shape=(
            jax.ShapeDtypeStruct((2, nr, SUB, sub_rows, width), BF16),
            jax.ShapeDtypeStruct((nr, rows, width), BF16),
            jax.ShapeDtypeStruct((2 * nr, half, out), BF16),
            jax.ShapeDtypeStruct((1, 128), F32),
        ),
        in_specs=[vmem] * 3,
        out_specs=(hbm, hbm, vmem, vmem),
        scratch_shapes=[
            pltpu.VMEM((nz, SUB, sub_rows, width), BF16),
            pltpu.VMEM((4, nx, SUB, sub_rows, width), BF16),
            pltpu.VMEM((rows, width), BF16),
            pltpu.VMEM((own + 8, out), BF16),
            pltpu.VMEM((nr, own + 8, out), BF16),
            pltpu.VMEM((width, out), F32),
            pltpu.VMEM((rows, out), F32),
            pltpu.VMEM((2, 2, half, out), BF16),
            pltpu.VMEM((ngroup, half, out), BF16),
            pltpu.VMEM((1, 128), F32),
            pltpu.VMEM((ngroup, 1, 128), F32),
            pltpu.VMEM((nfar, half, out), BF16),
            pltpu.VMEM((nfar, 1, 128), F32),
            dma((2, reach, SUB)),
            dma((2, reach, SUB)),
            dma((nz, SUB)),
            dma((4, nx, SUB)),
            dma((4, nx, 2, SUB)),
            dma((2, nr, SUB)),
            dma((2 * chips,)),
            dma((nr,)),
            dma((2,)),
            dma((2,)),
            dma((chips,)),
            dma((nr,)),
            dma((ngroup,)),
            dma((ngroup,)),
            dma((ngroup,)),
            dma((ngroup,)),
            dma((nfar,)),
            dma((nfar,)),
            dma((nfar,)),
            dma((nfar,)),
            dma((2 * nr,)),
            dma((2 * nr,)),
        ],
        compiler_params=pltpu.CompilerParams(collective_id=0, has_side_effects=True),
        name="exchange",
    )(activations, down_weight, keep_mask)


def products_kernel(samples, count, row_ref, col_ref, s_ref, q_ref, dw_ref, mask_ref, gram_ref, upd_ref, drop):
    part = pl.program_id(0)
    width = col_ref.shape[1]
    own = dw_ref.shape[0]
    row_count = lax.axis_size(ROW)
    r, c = lax.axis_index(ROW), lax.axis_index(COL)
    mean_square = q_ref[...] / count + 1e-06
    damping = jnp.where(2 * r + part == c, 1.0, 0.0) * (damp_ratio * mean_square)
    eye = lax.broadcasted_iota(jnp.int32, (128, 128), 0) == lax.broadcasted_iota(jnp.int32, (128, 128), 1)
    extra = jnp.where(eye, jnp.broadcast_to(damping, (128, 128)), 0.0)
    over_rows = (((0,), (0,)), ((), ()))
    for tile in range(width // 128):
        low = tile * 128
        gram = lax.dot_general(row_ref[0, :, low : low + 128], col_ref[...], over_rows, preferred_element_type=F32)
        gram = gram * (1.0 / samples)
        gram_ref[low : low + 128, :] = gram.astype(BF16)
        gram_ref[low : low + 128, low : low + 128] = (gram[:, low : low + 128] + extra).astype(BF16)

    first = lax.rem(c, row_count) * own

    @pl.when(part == lax.div(c, row_count))
    def _():
        low = jnp.minimum(lax.div(first, 128) * 128, width - 256)
        window = row_ref[0, :, pl.ds(pl.multiple_of(low, 128), 256)]
        drop[...] = lax.dot_general(window, s_ref[...], over_rows, preferred_element_type=F32) * (1.0 / samples)
        descent = drop[pl.ds(pl.multiple_of(first - low, 8), own), :]
        scale = jnp.broadcast_to((1.0 + damp_ratio) * mean_square[:, 0:1], descent.shape)
        updated = dw_ref[...].astype(F32) + step_ratio * descent / scale
        upd_ref[...] = (mask_ref[...].astype(F32) * updated).astype(BF16)


def products(row_panels, col_panel, s, squares, down_weight, keep_mask, count):
    _, samples, width = row_panels.shape
    own, out = down_weight.shape

    def whole(shape):
        return pl.BlockSpec(shape, lambda part: (0,) * len(shape))

    return pl.pallas_call(
        functools.partial(products_kernel, samples, count),
        out_shape=(jax.ShapeDtypeStruct((2 * width, width), BF16), jax.ShapeDtypeStruct((own, out), BF16)),
        grid=(2,),
        in_specs=[
            pl.BlockSpec((1, samples, width), lambda part: (part, 0, 0)),
            whole(col_panel.shape),
            whole(s.shape),
            whole(squares.shape),
            whole(down_weight.shape),
            whole(keep_mask.shape),
        ],
        out_specs=(pl.BlockSpec((width, width), lambda part: (part, 0)), whole((own, out))),
        scratch_shapes=[pltpu.VMEM((256, out), F32)],
        name="products",
    )(row_panels, col_panel, s, squares, down_weight, keep_mask)


def local(activations, down_weight, keep_mask):
    rows, width = activations.shape
    samples = rows * lax.axis_size(ROW)
    out = down_weight.shape[1]
    row_panels, col_panel, s, squares = exchange(activations, down_weight, keep_mask)
    return products(
        row_panels.reshape(2, samples, width),
        col_panel.reshape(samples, width),
        s.reshape(samples, out),
        squares,
        down_weight,
        keep_mask,
        samples * width * lax.axis_size(COL),
    )


def solution(mesh):
    torus = Mesh(mesh.devices.reshape(2, 4, 2, 16, 2), AXES)
    in_specs = (P(ROW, COL), P(AXES, None), P(AXES, None))
    out_specs = (P(ROW, COL), P(AXES, None))
    return jax.shard_map(local, mesh=torus, in_specs=in_specs, out_specs=out_specs, check_vma=False)
```

```python
import functools

import jax
import jax.numpy as jnp
from jax import lax
from jax.experimental import pallas as pl
from jax.experimental.pallas import tpu as pltpu
from jax.sharding import Mesh
from jax.sharding import PartitionSpec as P

MESH = pl.DeviceIdType.MESH
AXES = ("row_0", "row_1", "row_2", "col_0", "col_1")
ROW = AXES[:3]
COL = AXES[3:]
F32 = jnp.float32
BF16 = jnp.bfloat16
SUB = 1
NEAR = 4
AFTER = {1: ("weights",), 2: ("partial",)}
LATER = {3: ("near", "columns")}

damp_ratio = 0.1
step_ratio = 0.25


def each(low, high, work):
    def step(i, carry):
        work(i)
        return carry

    lax.fori_loop(low, high, step, 0)


def exchange_kernel(
    nx,
    nz,
    a_ref,
    dw_ref,
    mask_ref,
    rowp_ref,
    colp_ref,
    s_ref,
    q_ref,
    zbuf,
    xbuf,
    abuf,
    pown,
    pbuf,
    pfull,
    spart,
    near_out,
    near_in,
    nearq_out,
    nearq_in,
    far_buf,
    farq_buf,
    ring_send,
    ring_recv,
    x_send,
    x_recv,
    row_send,
    row_recv,
    col_send,
    col_recv,
    perm_sem,
    pair_sem,
    pag_send,
    pag_recv,
    near_send,
    near_recv,
    nearq_send,
    nearq_recv,
    far_send,
    far_recv,
    farq_send,
    farq_recv,
    pln_send,
    pln_recv,
):
    nr = 4 * nx
    chips = 2 * nx
    own = dw_ref.shape[0]
    rows, width = a_ref.shape
    half = rows // 2
    sub_rows = rows // SUB
    yl, x, k, z, yh = (lax.axis_index(name) for name in AXES)
    chip = yl * nx + x
    r = chip * 2 + k
    plane = 2 * r + yh
    ngroup = 4 * NEAR
    nfar = nz // NEAR
    zl, zb = lax.rem(z, NEAR), lax.div(z, NEAR)
    mate = (k * NEAR + zl) * 2 + yh

    def dev(r_, z_, yh_):
        return dict(
            row_0=lax.div(r_, 2 * nx),
            row_1=lax.rem(lax.div(r_, 2), nx),
            row_2=lax.rem(r_, 2),
            col_0=z_,
            col_1=yh_,
        )

    def in_plane(flat):
        return dev(lax.div(flat, 2), z, lax.rem(flat, 2))

    def in_near(flat):
        return dev(2 * chip + lax.div(flat, 2 * NEAR), zb * NEAR + lax.rem(lax.div(flat, 2), NEAR), lax.rem(flat, 2))

    def remote(src, dst, send, recv, to):
        return pltpu.make_async_remote_copy(
            src_ref=src, dst_ref=dst, send_sem=send, recv_sem=recv, device_id=to, device_id_type=MESH
        )

    def arrived(dst, sem):
        pltpu.make_async_copy(dst, dst, sem).wait()

    t_r, t_yh = 2 * lax.rem(z, nz // 2) + yh, lax.div(z, nz // 2)
    target = dev(t_r, r, t_yh)
    source = dev(z, yh * (nz // 2) + lax.div(r, 2), lax.rem(r, 2))
    fixed = (t_r == r) & (r == z) & (t_yh == yh)

    barrier = pltpu.get_barrier_semaphore()

    def greet(to):
        pl.semaphore_signal(barrier, inc=1, device_id=to, device_id_type=MESH)

    greet(target)
    greet(source)
    greeted = 2
    each(1, nfar, lambda off: greet(dev(r, lax.rem(z + off * NEAR, nz), yh)))
    greeted += nfar - 1
    for off in (1, 2, nz - 2, nz - 1):
        greet(dev(r, lax.rem(z + off, nz), yh))
        greeted += 1
    for core in range(2):
        for to_yh in range(2):
            each(1, NEAR, lambda off: greet(dev(2 * chip + core, zb * NEAR + lax.rem(zl + off, NEAR), to_yh)))
            greeted += NEAR - 1
    each(1, 2 * nr, lambda off: greet(in_plane(lax.rem(plane + off, 2 * nr))))
    greeted += 2 * nr - 1

    pown[0:own, :] = dw_ref[...] * (1 - mask_ref[...]).astype(BF16)
    act = a_ref[...].astype(F32)
    square = jnp.sum(jnp.sum(act * act, axis=0, keepdims=True), axis=1, keepdims=True)
    square = jnp.broadcast_to(square, (8, 256))
    high = square.astype(BF16).astype(F32)
    middle = (square - high).astype(BF16).astype(F32)
    low = (square - high - middle).astype(BF16).astype(F32)
    line = lax.broadcasted_iota(jnp.int32, (8, 256), 0)
    zero = jnp.zeros((8, 256), F32)
    coded = jnp.where(line == 0, high, jnp.where(line == 1, middle, jnp.where(line == 2, low, zero)))
    pown[own : own + 8, :] = coded.astype(BF16)
    pfull[...] = jnp.zeros(pfull.shape, F32)

    pl.semaphore_wait(barrier, greeted)

    perm = remote(pown, pbuf.at[t_r], perm_sem.at[0], perm_sem.at[1], target)
    perm_here = pltpu.make_async_copy(pown, pbuf.at[r], perm_sem.at[1])

    @pl.when(jnp.logical_not(fixed))
    def _():
        perm.start()

    @pl.when(fixed)
    def _():
        perm_here.start()

    reach = (nz // 2, nz - 1 - nz // 2)

    def block_at(way, dist):
        return lax.rem(z + nz - dist, nz) if way == 0 else lax.rem(z + dist, nz)

    def piece(block, dist, sub):
        if dist == 0:
            return a_ref.at[pl.ds(pl.multiple_of(sub * sub_rows, sub_rows), sub_rows)]
        return zbuf.at[block, sub]

    def ring_copy(way, dist, sub):
        hop = 1 if dist % 2 else 2
        block = block_at(way, dist - hop)
        to = lax.rem(z + hop, nz) if way == 0 else lax.rem(z + nz - hop, nz)
        return remote(
            piece(block, dist - hop, sub),
            zbuf.at[block, sub],
            ring_send.at[way, dist - 1, sub],
            ring_recv.at[way, dist - 1, sub],
            dev(r, to, yh),
        )

    def ring_from(way, dist, sub):
        for further in (dist + 2, dist + 1):
            if further <= reach[way]:
                ring_copy(way, further, sub).start()

    def column(block):
        return lax.rem(lax.div(block, 2), nx)

    def place(block):
        return lax.div(block, 2 * nx) * 2 + lax.rem(block, 2)

    def row_copy(block, xs, sub, src, to_yh):
        rs = (yl * nx + xs) * 2 + k
        return remote(
            src,
            rowp_ref.at[yh, rs, sub],
            row_send.at[place(block), xs, to_yh, sub],
            row_recv.at[yh, rs, sub],
            dev(block, z, to_yh),
        )

    def deliver(block, xs, sub, src):
        def one(turn):
            to_yh = lax.rem(turn + k, 2)
            here = (block == r) & (yh == to_yh)

            @pl.when(jnp.logical_not(here))
            def _():
                row_copy(block, xs, sub, src, to_yh).start()

            @pl.when(here)
            def _():
                rs = (yl * nx + xs) * 2 + k
                pltpu.make_async_copy(src, rowp_ref.at[yh, rs, sub], row_recv.at[yh, rs, sub]).start()

        each(0, 2, one)

    def x_copy(block, dist, sub):
        return remote(
            piece(block, dist, sub),
            xbuf.at[place(block), x, sub],
            x_send.at[block, sub],
            x_recv.at[place(block), x, sub],
            dev((yl * nx + column(block)) * 2 + k, z, yh),
        )

    def spread(block, dist, sub):
        @pl.when(column(block) == x)
        def _():
            deliver(block, x, sub, piece(block, dist, sub))

        @pl.when(column(block) != x)
        def _():
            x_copy(block, dist, sub).start()

    def relay(block, sub):
        @pl.when(column(block) == x)
        def _():
            def one(off):
                xs = lax.rem(x + off, nx)
                held = xbuf.at[place(block), xs, sub]
                arrived(held, x_recv.at[place(block), xs, sub])
                deliver(block, xs, sub, held)

            each(1, nx, one)

    def col_copy(off):
        other = lax.rem(chip + off, chips)
        return remote(a_ref, colp_ref.at[r], col_send.at[off], col_recv.at[r], dev(2 * other + k, z, yh))

    def col_from(off):
        return 2 * lax.rem(chip + chips - off, chips) + k

    pair = dev(2 * chip + 1 - k, z, yh)

    def col_pass(off, src):
        rs = col_from(off)
        return remote(src, colp_ref.at[rs], col_send.at[chips + off], col_recv.at[rs], pair)

    col_own = pltpu.make_async_copy(a_ref, colp_ref.at[r], col_recv.at[r])
    pair_copy = remote(a_ref, abuf, pair_sem.at[0], pair_sem.at[1], pair)

    for sub in range(SUB):
        for way in range(2):
            ring_from(way, 0, sub)
    for sub in range(SUB):
        spread(z, 0, sub)
    pair_copy.start()
    each(1, chips, lambda off: col_copy(off).start())
    col_pass(0, a_ref).start()
    col_own.start()

    def ring_round(t):
        near, far = 2 * t + 1, 2 * t + 2
        for dist in (far, near):

            def one(sub):
                for way in range(2):
                    if dist <= reach[way]:
                        block = block_at(way, dist)
                        arrived(zbuf.at[block, sub], ring_recv.at[way, dist - 1, sub])
                        if dist == far:
                            ring_from(way, dist, sub)

            each(0, SUB, one)

    def spread_round(t):
        def one(sub):
            for dist in (2 * t + 2, 2 * t + 1):
                for way in range(2):
                    if dist <= reach[way]:
                        spread(block_at(way, dist), dist, sub)

        each(0, SUB, one)

    def relay_round(t):
        for dist in (2 * t, 2 * t - 1) if t else (0,):

            def one(sub):
                for way in range(2 if t else 1):
                    if dist <= reach[way]:
                        relay(block_at(way, dist), sub)

            each(0, SUB, one)

    def pag_copy(off):
        other = lax.rem(chip + off, chips)
        return remote(pbuf.at[r], pbuf.at[r], pag_send.at[off], pag_recv.at[r], dev(2 * other + k, z, yh))

    def weights():
        arrived(pbuf.at[r], perm_sem.at[1])
        each(1, chips, lambda off: pag_copy(off).start())

    def near_copy(off):
        to = lax.rem(mate + off, ngroup)
        src = near_out.at[lax.div(to, 2 * NEAR), lax.rem(to, 2)]
        return remote(src, near_in.at[mate], near_send.at[off], near_recv.at[mate], in_near(to))

    def nearq_copy(off):
        to = in_near(lax.rem(mate + off, ngroup))
        return remote(nearq_out, nearq_in.at[mate], nearq_send.at[off], nearq_recv.at[mate], to)

    def partial():
        total = pbuf[r, own : own + 8, 0:128].astype(F32)
        pfull[pl.ds(pl.multiple_of(r * own, 8), own), :] = pbuf[r, 0:own, :].astype(F32)
        for off in range(1, chips):
            rs = col_from(off)
            arrived(pbuf.at[rs], pag_recv.at[rs])
            pfull[pl.ds(pl.multiple_of(rs * own, 8), own), :] = pbuf[rs, 0:own, :].astype(F32)
            total = total + pbuf[rs, own : own + 8, 0:128].astype(F32)
        arrived(abuf, pair_sem.at[1])
        weight = pfull[...].astype(BF16)
        mine = jnp.dot(a_ref[...], weight, preferred_element_type=F32)
        other = jnp.dot(abuf[...], weight, preferred_element_type=F32)
        spart[...] = mine
        for to_yh in range(2):
            near_out[k, to_yh] = mine[to_yh * half : (to_yh + 1) * half].astype(BF16)
            near_out[1 - k, to_yh] = other[to_yh * half : (to_yh + 1) * half].astype(BF16)
        nearq_out[...] = jnp.sum(total, axis=0, keepdims=True)
        each(1, ngroup, lambda off: near_copy(off).start())
        each(1, ngroup, lambda off: nearq_copy(off).start())

    def far_copy(off):
        to = dev(r, lax.rem(z + off * NEAR, nz), yh)
        return remote(far_buf.at[zb], far_buf.at[zb], far_send.at[off], far_recv.at[zb], to)

    def farq_copy(off):
        to = dev(r, lax.rem(z + off * NEAR, nz), yh)
        return remote(farq_buf.at[zb], farq_buf.at[zb], farq_send.at[off], farq_recv.at[zb], to)

    def near():
        total = spart[pl.ds(pl.multiple_of(yh * half, 8), half), :]
        squares = nearq_out[...]
        for off in range(1, ngroup):
            other = lax.rem(mate + off, ngroup)
            arrived(near_in.at[other], near_recv.at[other])
            total = total + near_in[other].astype(F32)
        for off in range(1, ngroup):
            other = lax.rem(mate + off, ngroup)
            arrived(nearq_in.at[other], nearq_recv.at[other])
            squares = squares + nearq_in[other]
        far_buf[zb] = total.astype(BF16)
        farq_buf[zb] = squares
        for off in range(1, nfar):
            far_copy(off).start()
            farq_copy(off).start()

    def pln_copy(off):
        to = in_plane(lax.rem(plane + off, 2 * nr))
        return remote(s_ref.at[plane], s_ref.at[plane], pln_send.at[off], pln_recv.at[plane], to)

    def far():
        for off in range(1, nfar):
            other = lax.rem(zb + off, nfar)
            arrived(far_buf.at[other], far_recv.at[other])
            arrived(farq_buf.at[other], farq_recv.at[other])
        total = far_buf[0].astype(F32)
        squares = farq_buf[0]
        for other in range(1, nfar):
            total = total + far_buf[other].astype(F32)
            squares = squares + farq_buf[other]
        s_ref[plane] = total.astype(BF16)
        q_ref[...] = squares
        each(1, 2 * nr, lambda off: pln_copy(off).start())

    def columns():
        def one(off):
            rs = col_from(off)
            arrived(colp_ref.at[rs], col_recv.at[rs])
            col_pass(off, colp_ref.at[rs]).start()

        each(1, chips, one)

    stages = dict(weights=weights, partial=partial, near=near, far=far, columns=columns)
    done = []
    rounds = (reach[0] + 1) // 2
    for t in range(rounds):
        ring_round(t)
        for name in AFTER.get(t, ()):
            stages[name]()
            done.append(name)
        spread_round(t)
        relay_round(t)
        for name in LATER.get(t, ()):
            stages[name]()
            done.append(name)
    relay_round(rounds)
    for name in ("weights", "partial", "columns", "near", "far"):
        if name not in done:
            stages[name]()

    def wait_col(off):
        rs = 2 * lax.rem(chip + off, chips) + 1 - k
        arrived(colp_ref.at[rs], col_recv.at[rs])

    def wait_plane(off):
        other = lax.rem(plane + off, 2 * nr)
        arrived(s_ref.at[other], pln_recv.at[other])

    def wait_row(i):
        from_yh, rs = lax.div(i, nr), lax.rem(i, nr)
        for sub in range(SUB):
            arrived(rowp_ref.at[from_yh, rs, sub], row_recv.at[from_yh, rs, sub])

    each(0, chips, wait_col)
    col_own.wait()
    each(0, 2 * nr, wait_row)
    each(1, 2 * nr, wait_plane)

    @pl.when(jnp.logical_not(fixed))
    def _():
        perm.wait_send()

    def wait_ring(sub):
        for way in range(2):
            for dist in range(1, reach[way] + 1):
                ring_copy(way, dist, sub).wait_send()

    each(0, SUB, wait_ring)

    def wait_block(block):
        @pl.when(column(block) != x)
        def _():
            for sub in range(SUB):
                x_copy(block, 0, sub).wait_send()

        @pl.when(column(block) == x)
        def _():
            def one(i):
                xs, to_yh = lax.div(i, 2), lax.rem(i, 2)

                @pl.when(jnp.logical_not((r == block) & (yh == to_yh)))
                def _():
                    for sub in range(SUB):
                        row_copy(block, xs, sub, piece(block, 0, sub), to_yh).wait_send()

            each(0, 2 * nx, one)

    each(0, nz, wait_block)

    def wait_chip(off):
        col_copy(off).wait_send()
        pag_copy(off).wait_send()

    def wait_near(off):
        near_copy(off).wait_send()
        nearq_copy(off).wait_send()

    def wait_far(off):
        far_copy(off).wait_send()
        farq_copy(off).wait_send()

    pair_copy.wait_send()
    each(1, chips, wait_chip)
    each(0, chips, lambda off: arrived(a_ref, col_send.at[chips + off]))
    each(1, ngroup, wait_near)
    each(1, nfar, wait_far)
    each(1, 2 * nr, lambda off: pln_copy(off).wait_send())


def exchange(activations, down_weight, keep_mask):
    nx = lax.axis_size("row_1")
    nz = lax.axis_size("col_0")
    nr = 4 * nx
    chips = 2 * nx
    rows, width = activations.shape
    own, out = down_weight.shape
    half = rows // 2
    sub_rows = rows // SUB
    reach = nz // 2
    ngroup = 4 * NEAR
    nfar = nz // NEAR
    dma = pltpu.SemaphoreType.DMA
    vmem = pl.BlockSpec(memory_space=pltpu.VMEM)
    hbm = pl.BlockSpec(memory_space=pl.ANY)
    return pl.pallas_call(
        functools.partial(exchange_kernel, nx, nz),
        out_shape=(
            jax.ShapeDtypeStruct((2, nr, SUB, sub_rows, width), BF16),
            jax.ShapeDtypeStruct((nr, rows, width), BF16),
            jax.ShapeDtypeStruct((2 * nr, half, out), BF16),
            jax.ShapeDtypeStruct((1, 128), F32),
        ),
        in_specs=[vmem] * 3,
        out_specs=(hbm, hbm, vmem, vmem),
        scratch_shapes=[
            pltpu.VMEM((nz, SUB, sub_rows, width), BF16),
            pltpu.VMEM((4, nx, SUB, sub_rows, width), BF16),
            pltpu.VMEM((rows, width), BF16),
            pltpu.VMEM((own + 8, out), BF16),
            pltpu.VMEM((nr, own + 8, out), BF16),
            pltpu.VMEM((width, out), F32),
            pltpu.VMEM((rows, out), F32),
            pltpu.VMEM((2, 2, half, out), BF16),
            pltpu.VMEM((ngroup, half, out), BF16),
            pltpu.VMEM((1, 128), F32),
            pltpu.VMEM((ngroup, 1, 128), F32),
            pltpu.VMEM((nfar, half, out), BF16),
            pltpu.VMEM((nfar, 1, 128), F32),
            dma((2, reach, SUB)),
            dma((2, reach, SUB)),
            dma((nz, SUB)),
            dma((4, nx, SUB)),
            dma((4, nx, 2, SUB)),
            dma((2, nr, SUB)),
            dma((2 * chips,)),
            dma((nr,)),
            dma((2,)),
            dma((2,)),
            dma((chips,)),
            dma((nr,)),
            dma((ngroup,)),
            dma((ngroup,)),
            dma((ngroup,)),
            dma((ngroup,)),
            dma((nfar,)),
            dma((nfar,)),
            dma((nfar,)),
            dma((nfar,)),
            dma((2 * nr,)),
            dma((2 * nr,)),
        ],
        compiler_params=pltpu.CompilerParams(collective_id=0, has_side_effects=True),
        name="exchange",
    )(activations, down_weight, keep_mask)


def products_kernel(samples, count, row_ref, col_ref, s_ref, q_ref, dw_ref, mask_ref, gram_ref, upd_ref, drop):
    part = pl.program_id(0)
    width = col_ref.shape[1]
    own = dw_ref.shape[0]
    row_count = lax.axis_size(ROW)
    r, c = lax.axis_index(ROW), lax.axis_index(COL)
    mean_square = q_ref[...] / count + 1e-06
    damping = jnp.where(2 * r + part == c, 1.0, 0.0) * (damp_ratio * mean_square)
    eye = lax.broadcasted_iota(jnp.int32, (128, 128), 0) == lax.broadcasted_iota(jnp.int32, (128, 128), 1)
    extra = jnp.where(eye, jnp.broadcast_to(damping, (128, 128)), 0.0)
    over_rows = (((0,), (0,)), ((), ()))
    for tile in range(width // 128):
        low = tile * 128
        gram = lax.dot_general(row_ref[0, :, low : low + 128], col_ref[...], over_rows, preferred_element_type=F32)
        gram = gram * (1.0 / samples)
        gram_ref[low : low + 128, :] = gram.astype(BF16)
        gram_ref[low : low + 128, low : low + 128] = (gram[:, low : low + 128] + extra).astype(BF16)

    first = lax.rem(c, row_count) * own

    @pl.when(part == lax.div(c, row_count))
    def _():
        low = jnp.minimum(lax.div(first, 128) * 128, width - 256)
        window = row_ref[0, :, pl.ds(pl.multiple_of(low, 128), 256)]
        drop[...] = lax.dot_general(window, s_ref[...], over_rows, preferred_element_type=F32) * (1.0 / samples)
        descent = drop[pl.ds(pl.multiple_of(first - low, 8), own), :]
        scale = jnp.broadcast_to((1.0 + damp_ratio) * mean_square[:, 0:1], descent.shape)
        updated = dw_ref[...].astype(F32) + step_ratio * descent / scale
        upd_ref[...] = (mask_ref[...].astype(F32) * updated).astype(BF16)


def products(row_panels, col_panel, s, squares, down_weight, keep_mask, count):
    _, samples, width = row_panels.shape
    own, out = down_weight.shape

    def whole(shape):
        return pl.BlockSpec(shape, lambda part: (0,) * len(shape))

    return pl.pallas_call(
        functools.partial(products_kernel, samples, count),
        out_shape=(jax.ShapeDtypeStruct((2 * width, width), BF16), jax.ShapeDtypeStruct((own, out), BF16)),
        grid=(2,),
        in_specs=[
            pl.BlockSpec((1, samples, width), lambda part: (part, 0, 0)),
            whole(col_panel.shape),
            whole(s.shape),
            whole(squares.shape),
            whole(down_weight.shape),
            whole(keep_mask.shape),
        ],
        out_specs=(pl.BlockSpec((width, width), lambda part: (part, 0)), whole((own, out))),
        scratch_shapes=[pltpu.VMEM((256, out), F32)],
        name="products",
    )(row_panels, col_panel, s, squares, down_weight, keep_mask)


def local(activations, down_weight, keep_mask):
    rows, width = activations.shape
    samples = rows * lax.axis_size(ROW)
    out = down_weight.shape[1]
    row_panels, col_panel, s, squares = exchange(activations, down_weight, keep_mask)
    return products(
        row_panels.reshape(2, samples, width),
        col_panel.reshape(samples, width),
        s.reshape(samples, out),
        squares,
        down_weight,
        keep_mask,
        samples * width * lax.axis_size(COL),
    )


def solution(mesh):
    torus = Mesh(mesh.devices.reshape(2, 4, 2, 16, 2), AXES)
    in_specs = (P(ROW, COL), P(AXES, None), P(AXES, None))
    out_specs = (P(ROW, COL), P(AXES, None))
    return jax.shard_map(local, mesh=torus, in_specs=in_specs, out_specs=out_specs, check_vma=False)
```
